32 devices in a mesh: gx: 4 (over y, core), gy: 4 (over z), gz: 2 (over x).
Axes of the slice: x: 2, y: 2, z: 4, core: 2. Of those that a mesh axis runs over, the one named last changes fastest.
Arguments:
- positions: float32 [3, 4, 4, 2, 192], P(None, 'gx', 'gy', 'gz'), may hold values from 0 to 8, as said below
- polarizability: float32 [4, 4, 2, 192], P('gx', 'gy', 'gz'), may hold values from 0.01 to 0.06
- direct_field: float32 [3, 4, 4, 2, 192], P(None, 'gx', 'gy', 'gz'), may hold values from -150 to 150
- groups: int32 [4, 4, 2, 192], P('gx', 'gy', 'gz'), may hold values from 0 to 47, never falling along the last dimension, each value on 1 to 8 neighbouring positions
Outputs:
- dipoles: float32 [3, 4, 4, 2, 192], P(None, 'gx', 'gy', 'gz')
- gradient: float32 [3, 4, 4, 2, 192], P(None, 'gx', 'gy', 'gz')
- energy: float32 [], replicated
The draws below stay inside these ranges and needn't reach their ends.
Inputs may be any that keep to these rules, and one draw needn't show every extreme that they name: `positions`: atoms of a domain sit one to a lattice site of 8 x 8 x 3 sites of spacing 1, in the order x, y, normal (the normal fastest), each within 0.2 of its site along every component, so no two atoms are closer than 0.6. `groups`: along the atoms of one domain the ids never fall; each group holds 1 to 8 atoms.
All inputs are finite; a program needn't handle non-finite values.
Results may differ from the reference program's by a relative error of at most 0.0003.
Values sent between devices are 32-bit elements; how exact they have to be, the bound alone decides.
A program may use at most 64 MiB of HBM per device.

```python
import math
import jax
import jax.numpy as jnp
import numpy as np
from jax import lax

LX = 8
LY = 8
DEPTH = 3
CUTOFF = 3
ATOMS_DEV = 192
ATOMS = 6144
N_GX = 4
N_GY = 4
N_GZ = 2
DEVICES = 32


def draw_positions(key, part):
    atom_count = LX * LY * DEPTH
    site_ids = jnp.arange(atom_count, dtype=jnp.int32)
    lattice = jnp.stack([site_ids // (LY * DEPTH), site_ids // DEPTH % LY, site_ids % DEPTH]).astype(jnp.float32) + 0.5
    reach = 0.15
    jitter = jax.random.uniform(key, (3, N_GX, N_GY, N_GZ, atom_count), minval=-reach, maxval=reach)
    return lattice[:, None, None, None, :] + jitter


def draw_direct_field(key, part):
    atom_count = LX * LY * DEPTH
    domain_ids = jnp.arange(DEVICES, dtype=jnp.int32).reshape(N_GX, N_GY, N_GZ).astype(jnp.float32)
    ramp_up = domain_ids / (DEVICES - 1)
    spread = (12.0 * (1.0 + 2.0 * ramp_up))[None, :, :, :, None]
    full_shape = (3, N_GX, N_GY, N_GZ, atom_count)
    values = jnp.clip(jax.random.normal(key, full_shape), -4.0, 4.0) * spread
    return values


def block_levels(key, shape, shards, least, largest):
    def one(axis_at, shards_of):
        draws = jax.random.uniform(jax.random.fold_in(jax.random.fold_in(key, 6), axis_at), (shards_of,), jnp.float32, least / len(shards), largest / len(shards))
        return jnp.repeat(jnp.exp(draws), shape[axis_at] // shards_of).reshape((-1,) + (1,) * (len(shape) - axis_at - 1))

    gain = one(*shards[0])
    for cut in shards[1:]:
        gain = gain * one(*cut)
    return gain


def split_up(count, total, most, slope):
    portions = [(1 << 20) // math.isqrt(grade ** slope) + 1 for grade in range(2, count + 1)]
    spare, holding = total - most - (count - 1), [1] * (count - 1)
    while spare > 0:
        free = [i for i in range(count - 1) if holding[i] < most]
        pool, budget = sum([portions[i] for i in free]), spare
        for i in free:
            addition = min(most - holding[i], max(1, budget * portions[i] // pool), spare)
            holding[i] = holding[i] + addition
            spare = spare - addition
    return np.array([most] + holding)


def uneven(own_key, count, total, most, lean):
    if count == 2:
        one = jax.random.randint(own_key, (), max(1, total - most), min(most, total - 1) + 1)
        return jnp.stack([one, total - one])
    sizes = jnp.asarray(split_up(count, total, most, lean), jnp.int32)
    twos = (count - 1) // 2
    donor, sink = sizes[1:1 + 2 * twos:2], sizes[2:2 + 2 * twos:2]
    margin = jnp.minimum(donor - 1, most - sink)
    passed = jax.random.randint(jax.random.fold_in(own_key, 1), (twos,), 0, 1 << 20) % (margin + 1)
    sizes = sizes.at[1:1 + 2 * twos:2].set(donor - passed).at[2:2 + 2 * twos:2].set(sink + passed)
    return sizes[jax.random.permutation(jax.random.fold_in(own_key, 2), count)]


def setup_inputs(seed: int = 0) -> dict:
    key_of = jax.random.split(jax.random.key(seed), 5)
    return {
        "positions": draw_positions(jax.random.fold_in(key_of[4], 71), 0),
        "polarizability": jnp.clip(jnp.exp(math.log(0.06) - 1.7917595 * jax.random.uniform(key_of[1], (N_GX, N_GY, N_GZ, ATOMS_DEV), jnp.float32) ** block_levels(key_of[1], (N_GX, N_GY, N_GZ, ATOMS_DEV), ((0, 4), (1, 4), (2, 2)), -0.2, 0.2)), 0.01, 0.06),
        "direct_field": draw_direct_field(jax.random.fold_in(key_of[4], 71), 0),
        "groups": jax.vmap(lambda own: jnp.searchsorted(jnp.cumsum(uneven(own, ATOMS_DEV // 4, ATOMS_DEV, 8, 1)), jnp.arange(ATOMS_DEV), side="right"))(jax.random.split(key_of[3], N_GX * N_GY * N_GZ)).reshape((N_GX, N_GY, N_GZ, ATOMS_DEV)).astype(jnp.int32),
    }


thole_factor = 0.39
group_scale = 0.5

def tensor_parts(own_pos, own_polar, own_group, far_pos, far_polar, centre):
    atom_count = own_pos.shape[1]
    displace = far_pos[:, None, :] - own_pos[:, :, None]
    dist_sq = lax.optimization_barrier(jnp.sum(displace * displace, axis=0))
    same_atom = jnp.logical_and(centre, jnp.eye(atom_count, dtype=bool))
    same_group = jnp.logical_and(centre, own_group[:, None] == own_group[None, :])
    safe_sq = jnp.where(same_atom, 1.0, dist_sq)
    inverse = lax.rsqrt(safe_sq)
    cut_ratio = safe_sq / (CUTOFF * CUTOFF)
    smooth_cut = jnp.where(cut_ratio < 1.0, jnp.square(1.0 - cut_ratio), 0.0)
    damping = thole_factor * safe_sq * safe_sq * inverse / jnp.sqrt(own_polar[:, None] * far_polar[None, :])
    decayed = jnp.exp(-damping)
    damp_three = -jnp.expm1(-damping)
    damp_five = damp_three - damping * decayed
    weight = smooth_cut * jnp.where(same_group, group_scale, 1.0) * jnp.where(same_atom, 0.0, 1.0)
    inv_cube = inverse * inverse * inverse
    coupling3 = weight * damp_three * inv_cube
    coupling5 = 3.0 * weight * damp_five * inv_cube * inverse * inverse
    return (displace, coupling3, coupling5)

def apply_tensor(own_pos, own_polar, own_group, far_pos, far_polar, far_vector, centre_flags):
    atom_count = own_pos.shape[1]

    def advance(running, slot_item):
        pos_slot, polar_slot, vector_slot, centre = slot_item
        displace, coupling3, coupling5 = tensor_parts(own_pos, own_polar, own_group, pos_slot, polar_slot, centre)
        along = lax.optimization_barrier(jnp.sum(displace * vector_slot[:, None, :], axis=0))
        contrib = lax.optimization_barrier(jnp.sum(coupling5[None] * displace * along[None] - coupling3[None] * vector_slot[:, None, :], axis=2))
        return (running + contrib, None)
    result, _ = lax.scan(advance, jnp.zeros((3, atom_count), jnp.float32), (far_pos, far_polar, far_vector, centre_flags))
    return result

def pair_gradient(own_pos, own_polar, own_group, far_pos, far_polar, own_dip, own_adj, far_dip, far_adj, centre_flags):

    def slot_value(position, pos_slot, polar_slot, dip_slot, adj_slot, centre):
        displace, coupling3, coupling5 = tensor_parts(position, own_polar, own_group, pos_slot, polar_slot, centre)
        own_dip_along = lax.optimization_barrier(jnp.sum(displace * own_dip[:, :, None], axis=0))
        own_adj_along = lax.optimization_barrier(jnp.sum(displace * own_adj[:, :, None], axis=0))
        far_dip_along = lax.optimization_barrier(jnp.sum(displace * dip_slot[:, None, :], axis=0))
        far_adj_along = lax.optimization_barrier(jnp.sum(displace * adj_slot[:, None, :], axis=0))
        cross_terms = lax.optimization_barrier(jnp.sum(own_dip[:, :, None] * adj_slot[:, None, :] + own_adj[:, :, None] * dip_slot[:, None, :], axis=0))
        return 0.5 * jnp.sum(coupling5 * (own_dip_along * far_adj_along + own_adj_along * far_dip_along) - coupling3 * cross_terms)

    def advance(running, slot_item):
        pos_slot, polar_slot, dip_slot, adj_slot, centre = slot_item
        return (running + jax.grad(slot_value)(own_pos, pos_slot, polar_slot, dip_slot, adj_slot, centre), None)
    result, _ = lax.scan(advance, jnp.zeros(own_pos.shape, jnp.float32), (far_pos, far_polar, far_dip, far_adj, centre_flags))
    return result

def slot_table():
    slot_ids = jnp.arange(27, dtype=jnp.int32)
    shifts = jnp.stack([(slot_ids // 9 - 1) * LX, (slot_ids // 3 % 3 - 1) * LY, (slot_ids % 3 - 1) * DEPTH], axis=1).astype(jnp.float32)
    return (shifts, slot_ids == 13)

def wrap_pad(array):
    return jnp.pad(array, ((0, 0), (1, 1), (1, 1), (1, 1), (0, 0)), mode='wrap')

def neighbourhood(padded, flat_index):
    channels = padded.shape[0]
    atom_count = padded.shape[-1]
    index_x = flat_index // (N_GY * N_GZ)
    index_y = flat_index // N_GZ % N_GY
    index_z = flat_index % N_GZ
    zero = jnp.zeros((), jnp.int32)
    block = lax.dynamic_slice(padded, (zero, index_x, index_y, index_z, zero), (channels, 3, 3, 3, atom_count))
    return block.reshape(channels, 27, atom_count).transpose(1, 0, 2)

def reference(positions, polarizability, direct_field, groups):
    full_shape = positions.shape
    frame = jnp.concatenate([positions, polarizability[None]], axis=0)
    padded_frame = wrap_pad(frame)
    own_pos_all = positions.reshape(3, DEVICES, -1)
    polar = polarizability.reshape(DEVICES, -1)
    group_all = groups.reshape(DEVICES, -1)
    direct = direct_field.reshape(3, DEVICES, -1)
    shifts, centre_flags = slot_table()
    flat_ids = jnp.arange(DEVICES, dtype=jnp.int32)

    def local_frame(flat_index):
        slots = neighbourhood(padded_frame, flat_index)
        return (slots[:, :3] + shifts[:, :, None], slots[:, 3])

    def apply_all(vector):
        padded_vec = wrap_pad(vector.reshape(full_shape))

        def one_device(flat_index):
            far_pos, far_polar = local_frame(flat_index)
            return apply_tensor(own_pos_all[:, flat_index], polar[flat_index], group_all[flat_index], far_pos, far_polar, neighbourhood(padded_vec, flat_index), centre_flags)
        return lax.map(one_device, flat_ids).transpose(1, 0, 2)
    dipole_start = polar * direct
    resid_start = apply_all(dipole_start)
    precond_start = polar * resid_start
    search_first = precond_start
    norm_first = jnp.sum(resid_start * precond_start)
    image_first = search_first / polar - apply_all(search_first)
    gamma_first = norm_first / jnp.sum(search_first * image_first)
    dipole_mid = dipole_start + gamma_first * search_first
    resid_mid = resid_start - gamma_first * image_first
    precond_mid = polar * resid_mid
    norm_mid = jnp.sum(resid_mid * precond_mid)
    search_second = precond_mid + norm_mid / norm_first * search_first
    image_second = search_second / polar - apply_all(search_second)
    gamma_second = norm_mid / jnp.sum(search_second * image_second)
    dipoles = dipole_mid + gamma_second * search_second
    energy = -jnp.sum(dipoles * direct) / (2.0 * ATOMS)
    adjoint = polar * direct + polar * apply_all(dipoles)
    padded_dip = wrap_pad(dipoles.reshape(full_shape))
    padded_adj = wrap_pad(adjoint.reshape(full_shape))

    def grad_device(flat_index):
        far_pos, far_polar = local_frame(flat_index)
        return pair_gradient(own_pos_all[:, flat_index], polar[flat_index], group_all[flat_index], far_pos, far_polar, dipoles[:, flat_index], adjoint[:, flat_index], neighbourhood(padded_dip, flat_index), neighbourhood(padded_adj, flat_index), centre_flags)
    gradient = lax.map(grad_device, flat_ids).transpose(1, 0, 2)
    return (dipoles.reshape(full_shape), gradient.reshape(full_shape), energy)
```

```python
import functools

import jax
import jax.numpy as jnp
from jax import lax
from jax.experimental import pallas as pl
from jax.experimental.pallas import tpu as pltpu
from jax.sharding import PartitionSpec as P

MESH = pl.DeviceIdType.MESH
LX, LY, DEPTH, CUT = 8, 8, 3, 3
WY = LY + 2 * CUT
SPAN = DEPTH * WY
HOME = CUT * WY + CUT
LANES = 128
F32 = jnp.float32
LOOPS = ((-1, 1, 3, 3), (-2, 4, 2, 2), (-3, 6, 2, 1))
PAIRS = sum(n * (2 * w + 1) * 3 for _, _, n, w in LOOPS)
TXX, TXY, TXZ, TYY, TYZ, TZZ, DX, DY, DZ, C5, H3, H5 = range(12)
EXCH = 4


def lane_roll(x, shift):
    shift = shift % LANES
    return x if shift == 0 else pltpu.roll(x, shift, axis=1)


def canon(o, n):
    return o % n if n <= 2 else o


def halo_offsets(dims):
    out = []
    for ox in (-1, 0, 1):
        for oy in (-1, 0, 1):
            for oz in (-1, 0, 1):
                c = tuple(canon(o, n) for o, n in zip((ox, oy, oz), dims))
                if c != (0, 0, 0) and c not in out:
                    out.append(c)
    return out


def kernel(dims, devices, pos_ref, pol_ref, dir_ref, grp_ref, dip_ref, grad_ref, en_ref,
           sbf, sbv, rbf, rbv, red, vpad, vd, pd, own, tab,
           sf_send, sf_recv, sv_send, sv_recv, r_send, r_recv, q_send, q_recv, red2, rsb):
    nx, ny, nz = dims
    me = (lax.axis_index("gx"), lax.axis_index("gy"), lax.axis_index("gz"))

    def at(o):
        return tuple(lax.rem(m + (k % n), n) for m, k, n in zip(me, o, dims))

    halo = halo_offsets(dims)
    plane = [(x, 0, z) for x in range(nx) for z in range(nz) if (x, z) != (0, 0)]
    column = [(0, y, 0) for y in range(1, ny)]
    partners = []
    for o in halo + plane + column:
        m = tuple(k % n for k, n in zip(o, dims))
        if m not in partners:
            partners.append(m)
    barrier = pltpu.get_barrier_semaphore()
    for o in partners:
        pl.semaphore_signal(barrier, inc=1, device_id=at(o), device_id_type=MESH)

    lane = lax.broadcasted_iota(jnp.int32, (8, LANES), 1)
    row = lax.broadcasted_iota(jnp.int32, (8, LANES), 0)
    lane_f = lane.astype(F32)
    zl = jnp.floor((lane_f + 0.5) * (1.0 / WY))
    yl = lane_f - WY * zl
    home = (zl >= CUT) & (zl < CUT + DEPTH) & (yl >= CUT) & (yl < CUT + LY)
    atoms = LX * LY * DEPTH
    i_col = lax.broadcasted_iota(jnp.int32, (atoms, LANES), 0).astype(F32)
    l_col = lax.broadcasted_iota(jnp.int32, (atoms, LANES), 1).astype(F32)
    rest = i_col - (LY * DEPTH) * jnp.floor((i_col + 0.5) * (1.0 / (LY * DEPTH)))
    y_col = jnp.floor((rest + 0.5) * (1.0 / DEPTH))
    z_col = rest - DEPTH * y_col
    place = jnp.where(l_col == WY * z_col + y_col + HOME, 1.0, 0.0)
    i_row = lax.broadcasted_iota(jnp.int32, (8, atoms), 1).astype(F32)
    x_row = lax.broadcasted_iota(jnp.int32, (8, atoms), 0).astype(F32)
    pick = jnp.floor((i_row + 0.5) * (1.0 / (LY * DEPTH))) == x_row
    raw = [pos_ref[c:c + 1, :] for c in range(3)] + [dir_ref[c:c + 1, :] for c in range(3)]
    raw += [pol_ref[...], grp_ref[...].astype(F32)]
    stack = jnp.concatenate([jnp.where(pick, jnp.broadcast_to(r, (8, atoms)), 0.0) for r in raw], axis=0)
    spread = jnp.dot(stack, place, precision=lax.Precision.HIGHEST, preferred_element_type=F32)
    field = [spread[8 * k:8 * k + 8] for k in range(8)]
    site = (row.astype(F32), yl - CUT, zl - CUT)
    u = [jnp.where(home, field[c] - site[c], 0.0) for c in range(3)]
    direct = field[3:6]
    pol, group = field[6], field[7]
    d0 = [pol * f for f in direct]

    def pack(parts):
        out = None
        for c, p in enumerate(parts):
            r = lane_roll(p, SPAN * c - HOME)
            out = r if out is None else out + r
        return out

    sbf[0] = pack(u)
    sbf[1] = pack(d0)
    sbf[2] = pack([pol])
    pl.semaphore_wait(barrier, len(partners))

    def halo_copies(k):
        for j, o in enumerate(halo):
            back = at(tuple(-v for v in o))
            if k == 0:
                yield pltpu.make_async_remote_copy(sbf, rbf.at[j], sf_send.at[j], sf_recv.at[j],
                                                   device_id=back, device_id_type=MESH)
            else:
                yield pltpu.make_async_remote_copy(sbv.at[k - 1], rbv.at[k - 1, j], sv_send.at[k - 1, j],
                                                   sv_recv.at[k - 1, j], device_id=back, device_id_type=MESH)

    def start(copies):
        copies = list(copies)
        for c in copies:
            c.start()
        return copies

    def block(k, tile, o):
        c = tuple(canon(v, n) for v, n in zip(o, dims))
        if c == (0, 0, 0):
            return sbf[tile] if k == 0 else sbv[k - 1]
        j = halo.index(c)
        return rbf[j, tile] if k == 0 else rbv[k - 1, j]

    low = row < CUT

    def assemble(k, tile, count, fill=0.0):
        out = [[jnp.full((8, LANES), fill, F32)] * 2 for _ in range(count)]
        done = {}
        for oy in (-1, 0, 1):
            y0, y1 = (0, CUT) if oy < 0 else (CUT, CUT + LY) if oy == 0 else (CUT + LY, WY)
            for oz in (-1, 0, 1):
                key = (oy if ny > 2 else oy % ny, oz if nz > 2 else oz % nz)
                if key not in done:
                    left, mid, right = (pltpu.roll(block(k, tile, (ox, oy, oz)), CUT, axis=0) for ox in (-1, 0, 1))
                    done[key] = (jnp.where(low, left, mid), jnp.where(low, mid, right))
                mask = (zl >= DEPTH * (oz + 1)) & (zl < DEPTH * (oz + 2)) & (yl >= y0) & (yl < y1)
                for c in range(count):
                    shift = SPAN * (oz + 1 - c) + LY * oy + CUT
                    for t in range(2):
                        out[c][t] = jnp.where(mask, lane_roll(done[key][t], shift), out[c][t])
        return out

    def spread_dy(ref, slot, tiles, add_dy=False):
        for dy in range(-CUT, CUT + 1):
            for t in range(2):
                v = lane_roll(tiles[t], -dy)
                ref[dy + CUT, slot, 8 * t:8 * t + 8, :] = v + float(dy) if add_dy else v

    def replicate(v):
        v = jnp.where(home, v, 0.0)
        base = v + lane_roll(v, SPAN) + lane_roll(v, -SPAN)
        return base, lane_roll(base, -WY), lane_roll(base, WY)

    def fold(acc):
        out = None
        for dz in range(-CUT, CUT + 1):
            r = lane_roll(acc[-dz % 3], -WY * dz)
            out = r if out is None else out + r
        return jnp.where(home, out, 0.0)

    def pair_loops(body):
        carry = tuple(jnp.zeros((8, LANES), F32) for _ in range(9))
        base = 0
        for first, step, n, w in LOOPS:
            width = (2 * w + 1) * 3

            def turn(it, carry, first=first, step=step, w=w, width=width, base=base):
                dyi = first + CUT + step * it
                carry = list(carry)
                for j, dx in enumerate(range(-w, w + 1)):
                    for q, add in enumerate(body(dx, dyi, base + it * width + 3 * j)):
                        for c in range(3):
                            carry[3 * q + c] = carry[3 * q + c] + add[c]
                return tuple(carry)

            carry = lax.fori_loop(0, n, turn, carry)
            base += n * width
        return [fold([carry[3 * q + c] for q in range(3)]) for c in range(3)]

    copies = start(halo_copies(0))
    dzq = (jnp.where(lane < SPAN, -3.0, jnp.where(lane < 2 * SPAN, 0.0, 3.0)),
           jnp.where(lane < 5 * WY, -1.0, 2.0), jnp.where(lane < 4 * WY, -2.0, 1.0))
    rp = lax.rsqrt(jnp.where(home, pol, 1.0))
    for c, v in enumerate(u + [rp, group]):
        for q, r in enumerate(replicate(v)):
            own[q, c] = r - dzq[q] if c == 2 else r
    far_group = [pltpu.roll(jnp.where(home, group, -1.0), CUT, axis=0)] * 2
    spread_dy(pd, 4, [jnp.where(low, -1.0, far_group[0]), jnp.where(low, far_group[1], -1.0)])
    for c in copies:
        c.wait()
    for c, tiles in enumerate(assemble(0, 0, 3)):
        spread_dy(pd, c, tiles, add_dy=c == 1)
    far_pol = assemble(0, 2, 1, 1.0)[0]
    spread_dy(pd, 3, [lax.rsqrt(jnp.where(t > 0.0, t, 1.0)) for t in far_pol])

    def keep(k, parts):
        for c, tiles in enumerate(parts):
            for t in range(2):
                vpad[k, c, t] = tiles[t]

    def ghosts(k):
        parts = assemble(k, 1 if k == 0 else 0, 3)
        keep(k, parts)
        for c in range(3):
            spread_dy(vd, c, parts[c])

    def rows(ref, dyi, slot, dx):
        return ref[dyi, slot, CUT + dx:CUT + dx + 8, :]

    def mul(t, v):
        xx, xy, xz, yy, yz, zz = t
        return (xx * v[0] + xy * v[1] + xz * v[2], xy * v[0] + yy * v[1] + yz * v[2],
                xz * v[0] + yz * v[1] + zz * v[2])

    def build(dx, dyi, index):
        far = [rows(pd, dyi, c, dx) for c in range(5)]
        v = [rows(vd, dyi, c, dx) for c in range(3)]
        out = []
        for q in range(3):
            ex = far[0] - own[q, 0] + float(dx)
            ey = far[1] - own[q, 1]
            ez = far[2] - own[q, 2]
            s = ex * ex + ey * ey + ez * ez
            same = s < 0.01
            maybe_self = dx == 0 and q == 0
            if maybe_self:
                s = jnp.where(same, 1.0, s)
            inv = lax.rsqrt(s)
            tap = jnp.maximum(1.0 - s * (1.0 / (CUT * CUT)), 0.0)
            x = (0.39 * s) * (s * inv) * (far[3] * own[q, 3])
            e = jnp.exp(-x)
            xe = x * e
            l3 = 1.0 - e
            l5 = l3 - xe
            inv2 = inv * inv
            g = jnp.where(far[4] == own[q, 4], 0.5, 1.0) * (inv2 * inv)
            if maybe_self:
                g = jnp.where(same, 0.0, g)
            gt = g * tap
            gi = 3.0 * gt * inv2
            gl = gt * l3
            c3 = gl * tap
            c5 = gi * tap * l5
            h3 = (-4.0 / (CUT * CUT)) * gl - c5
            h5 = gi * ((-4.0 / (CUT * CUT)) * l5 + tap * inv2 * (3.0 * x * xe - 5.0 * l5))
            fx, fy, fz = c5 * ex, c5 * ey, c5 * ez
            t = (fx * ex - c3, fx * ey, fx * ez, fy * ey - c3, fy * ez, fz * ez - c3)
            for k, value in enumerate(t + (ex, ey, ez, c5, h3, h5)):
                tab[k, index + q] = value
            out.append(mul(t, v))
        return out

    def apply(dx, dyi, index):
        v = [rows(vd, dyi, c, dx) for c in range(3)]
        return [mul([tab[k, index + q] for k in range(6)], v) for q in range(3)]

    def plane_id(o):
        p = at(o)
        return p[0] * nz + p[2]

    def begin_sum(r, values):
        tile = jnp.zeros((8, LANES), F32)
        for k, v in enumerate(values):
            total = jnp.sum(jnp.sum(v, axis=0, keepdims=True), axis=1, keepdims=True)
            tile = jnp.where(lane == k, total, tile)
        rsb[r, 0] = tile
        mine = me[0] * nz + me[2]
        copies = start(
            pltpu.make_async_remote_copy(rsb.at[r, 0], red.at[r, mine], r_send.at[r, j], r_recv.at[r, mine],
                                         device_id=at(o), device_id_type=MESH)
            for j, o in enumerate(plane))
        red[r, mine] = tile
        return copies

    def middle_sum(r, copies):
        for j, o in enumerate(plane):
            src = plane_id(o)
            pltpu.make_async_remote_copy(rsb.at[r, 0], red.at[r, src], r_send.at[r, j], r_recv.at[r, src],
                                         device_id=at(o), device_id_type=MESH).wait_recv()
        total = red[r, 0]
        for k in range(1, nx * nz):
            total = total + red[r, k]
        rsb[r, 1] = total
        out = start(
            pltpu.make_async_remote_copy(rsb.at[r, 1], red2.at[r, me[1]], q_send.at[r, j], q_recv.at[r, me[1]],
                                         device_id=at(o), device_id_type=MESH)
            for j, o in enumerate(column))
        red2[r, me[1]] = total
        for c in copies:
            c.wait_send()
        return out

    def end_sum(r, copies, count):
        for j, o in enumerate(column):
            src = at(o)[1]
            pltpu.make_async_remote_copy(rsb.at[r, 1], red2.at[r, src], q_send.at[r, j], q_recv.at[r, src],
                                         device_id=at(o), device_id_type=MESH).wait_recv()
        total = red2[r, 0]
        for k in range(1, ny):
            total = total + red2[r, k]
        for c in copies:
            c.wait_send()
        return [jnp.sum(jnp.where(lane == k, total, 0.0), axis=1, keepdims=True) for k in range(count)]

    def inner(a, b):
        return a[0] * b[0] + a[1] * b[1] + a[2] * b[2]

    ghosts(0)
    r0 = pair_loops(build)
    z0 = [pol * v for v in r0]
    sbv[0] = pack(z0)
    copies = start(halo_copies(1))
    for c in copies:
        c.wait()
    ghosts(1)
    t1 = pair_loops(apply)
    z2 = [pol * v for v in t1]
    sbv[1] = pack(z2)
    copies = start(halo_copies(2))
    image0 = [a - b for a, b in zip(r0, t1)]
    sums = begin_sum(0, [inner(r0, z0), inner(z0, image0), inner(d0, direct), inner(z0, direct)])
    sums = middle_sum(0, sums)
    for c in copies:
        c.wait()
    ghosts(2)
    t2 = pair_loops(apply)
    sbv[2] = pack([pol * v for v in t2])
    copies = start(halo_copies(3))
    norm0, curve0, e_d0, e_z0 = end_sum(0, sums, 4)
    gamma0 = norm0 / curve0
    r1 = [a - gamma0 * b for a, b in zip(r0, image0)]
    z1 = [pol * v for v in r1]
    tz1 = [a - gamma0 * (a - b) for a, b in zip(t1, t2)]
    az1 = [a - b for a, b in zip(r1, tz1)]
    sums = begin_sum(1, [inner(r1, z1), inner(z1, az1), inner(z1, image0), inner(z1, direct)])
    sums = middle_sum(1, sums)
    for c in copies:
        c.wait()
    keep(3, assemble(3, 0, 3))
    norm1, az11, az01, e_z1 = end_sum(1, sums, 4)
    beta = norm1 / norm0
    curve1 = az11 + 2.0 * beta * az01 + beta * beta * curve0
    gamma1 = norm1 / curve1
    energy = -(e_d0 + gamma0 * e_z0 + gamma1 * (e_z1 + beta * e_z0)) * (1.0 / (2.0 * atoms * devices))
    en_ref[...] = energy[0:1, :]

    own_p, own_a = [], []
    dip = []
    for c in range(3):
        dip.append(d0[c] + gamma0 * z0[c] + gamma1 * (z1[c] + beta * z0[c]))
        tiles_p, tiles_a = [], []
        for t in range(2):
            g0, g1, g2, g3 = (vpad[k, c, t] for k in range(4))
            f1 = g1 - gamma0 * (g1 - g2)
            f2 = g2 - gamma0 * (g2 - g3)
            tiles_p.append(g0 + gamma0 * g1 + gamma1 * (f1 + beta * g1))
            tiles_a.append(g0 + g1 + gamma0 * g2 + gamma1 * (f2 + beta * g2))
        spread_dy(vd, c, tiles_p)
        spread_dy(vd, 3 + c, tiles_a)
        for q, r in enumerate(replicate(dip[c])):
            own[q, 5 + c] = r
        for q, r in enumerate(replicate(vd[CUT, 3 + c, CUT:CUT + 8, :])):
            own[q, 8 + c] = r

    def slope(dx, dyi, index):
        fp = [rows(vd, dyi, c, dx) for c in range(3)]
        fa = [rows(vd, dyi, 3 + c, dx) for c in range(3)]
        out = []
        for q in range(3):
            op = [own[q, 5 + c] for c in range(3)]
            oa = [own[q, 8 + c] for c in range(3)]
            d = [tab[DX + c, index + q] for c in range(3)]
            opd, oad, fpd, fad = inner(op, d), inner(oa, d), inner(fp, d), inner(fa, d)
            cross = inner(op, fa) + inner(oa, fp)
            radial = tab[H5, index + q] * (opd * fad + oad * fpd) - tab[H3, index + q] * cross
            c5 = tab[C5, index + q]
            out.append(tuple(
                d[c] * radial + c5 * (op[c] * fad + fa[c] * opd + oa[c] * fpd + fp[c] * oad) for c in range(3)))
        return out

    grad = [-0.5 * v for v in pair_loops(slope)]
    result = lax.dot_general(jnp.concatenate(dip + grad, axis=0), place, (((1,), (1,)), ((), ())),
                             precision=lax.Precision.HIGHEST, preferred_element_type=F32)
    for c in range(6):
        line = jnp.sum(jnp.where(pick, result[8 * c:8 * c + 8], 0.0), axis=0, keepdims=True)
        if c < 3:
            dip_ref[c:c + 1, :] = line
        else:
            grad_ref[c - 3:c - 2, :] = line


def solution(mesh):
    dims = tuple(mesh.shape[a] for a in ("gx", "gy", "gz"))
    devices = dims[0] * dims[1] * dims[2]

    def on_device(positions, polarizability, direct_field, groups):
        atoms = positions.shape[-1]
        h = len(halo_offsets(dims))
        plane, column = dims[0] * dims[2], dims[1]
        dma = pltpu.SemaphoreType.DMA
        vmem = pl.BlockSpec(memory_space=pltpu.VMEM)
        dip, grad, energy = pl.pallas_call(
            functools.partial(kernel, dims, devices),
            out_shape=(jax.ShapeDtypeStruct((3, atoms), F32), jax.ShapeDtypeStruct((3, atoms), F32),
                       jax.ShapeDtypeStruct((1, 1), F32)),
            in_specs=[vmem] * 4,
            out_specs=(vmem, vmem, vmem),
            scratch_shapes=[
                pltpu.VMEM((3, 8, LANES), F32),
                pltpu.VMEM((EXCH - 1, 8, LANES), F32),
                pltpu.VMEM((h, 3, 8, LANES), F32),
                pltpu.VMEM((EXCH - 1, h, 8, LANES), F32),
                pltpu.VMEM((2, plane, 8, LANES), F32),
                pltpu.VMEM((EXCH, 3, 2, 8, LANES), F32),
                pltpu.VMEM((7, 6, 16, LANES), F32),
                pltpu.VMEM((7, 5, 16, LANES), F32),
                pltpu.VMEM((3, 11, 8, LANES), F32),
                pltpu.VMEM((12, PAIRS, 8, LANES), F32),
                dma((h,)), dma((h,)), dma((EXCH - 1, h)), dma((EXCH - 1, h)),
                dma((2, plane)), dma((2, plane)), dma((2, column)), dma((2, column)),
                pltpu.VMEM((2, column, 8, LANES), F32),
                pltpu.VMEM((2, 2, 8, LANES), F32),
            ],
            compiler_params=pltpu.CompilerParams(collective_id=0, has_side_effects=True),
        )(positions.reshape(3, atoms), polarizability.reshape(1, atoms), direct_field.reshape(3, atoms),
          groups.reshape(1, atoms))
        return dip.reshape(positions.shape), grad.reshape(positions.shape), energy.reshape(())

    vec, one = P(None, "gx", "gy", "gz", None), P("gx", "gy", "gz", None)
    return jax.shard_map(on_device, mesh=mesh, in_specs=(vec, one, vec, one), out_specs=(vec, vec, P()),
                         check_vma=False)
```

```python
import functools

import jax
import jax.numpy as jnp
from jax import lax
from jax.experimental import pallas as pl
from jax.experimental.pallas import tpu as pltpu
from jax.sharding import PartitionSpec as P

MESH = pl.DeviceIdType.MESH
LX, LY, DEPTH, CUT = 8, 8, 3, 3
WY = LY + 2 * CUT
SPAN = DEPTH * WY
HOME = CUT * WY + CUT
LANES = 128
F32 = jnp.float32
LOOPS = ((-1, 1, 3, 3), (-2, 4, 2, 2), (-3, 6, 2, 1))
PAIRS = sum(n * (2 * w + 1) * 3 for _, _, n, w in LOOPS)
TXX, TXY, TXZ, TYY, TYZ, TZZ, DX, DY, DZ, C5, H3, H5 = range(12)
EXCH = 4


def lane_roll(x, shift):
    shift = shift % LANES
    return x if shift == 0 else pltpu.roll(x, shift, axis=1)


def canon(o, n):
    return o % n if n <= 2 else o


def halo_offsets(dims):
    out = []
    for ox in (-1, 0, 1):
        for oy in (-1, 0, 1):
            for oz in (-1, 0, 1):
                c = tuple(canon(o, n) for o, n in zip((ox, oy, oz), dims))
                if c != (0, 0, 0) and c not in out:
                    out.append(c)
    return sorted(out, key=lambda c: -sum(map(abs, c)))


def sum_groups(dims):
    return ((0, 1, 2), ()) if dims[0] * dims[1] * dims[2] <= 32 else ((0, 2), (1,))


def group_offsets(dims, axes):
    sizes = [n if a in axes else 1 for a, n in enumerate(dims)]
    out = [(x, y, z) for x in range(sizes[0]) for y in range(sizes[1]) for z in range(sizes[2])]
    return sorted(out[1:], key=lambda o: -sum(min(k, n - k) for k, n in zip(o, dims)))


def group_size(dims, axes):
    return len(group_offsets(dims, axes)) + 1


def kernel(dims, devices, pos_hbm, pol_hbm, dir_hbm, grp_hbm, out_hbm, en_hbm,
           pos_ref, pol_ref, dir_ref, grp_ref, dip_ref, grad_ref, en_ref, io_sem, sbf, sbv, rbf, rbv, red, vpad, vd, pd, own, tab,
           sf_send, sf_recv, sv_send, sv_recv, r_send, r_recv, q_send, q_recv, red2, rsb, rsb2):
    nx, ny, nz = dims
    dip_hbm, grad_hbm = out_hbm.at[pl.ds(0, 3)], out_hbm.at[pl.ds(3, 3)]
    me = (lax.axis_index("gx"), lax.axis_index("gy"), lax.axis_index("gz"))

    def at(o):
        return tuple(lax.rem(m + (k % n), n) for m, k, n in zip(me, o, dims))

    halo = halo_offsets(dims)
    first, second = sum_groups(dims)
    plane = group_offsets(dims, first)
    column = group_offsets(dims, second)
    partners = []
    for o in halo + plane + column:
        m = tuple(k % n for k, n in zip(o, dims))
        if m not in partners:
            partners.append(m)
    barrier = pltpu.get_barrier_semaphore()
    for o in partners:
        pl.semaphore_signal(barrier, inc=1, device_id=at(o), device_id_type=MESH)
    loads = [pltpu.make_async_copy(a, b, io_sem.at[k]) for k, (a, b) in enumerate(
        ((pos_hbm, pos_ref), (dir_hbm, dir_ref), (pol_hbm, pol_ref), (grp_hbm, grp_ref)))]
    for c in loads:
        c.start()

    lane = lax.broadcasted_iota(jnp.int32, (8, LANES), 1)
    row = lax.broadcasted_iota(jnp.int32, (8, LANES), 0)
    lane_f = lane.astype(F32)
    zl = jnp.floor((lane_f + 0.5) * (1.0 / WY))
    yl = lane_f - WY * zl
    home = (zl >= CUT) & (zl < CUT + DEPTH) & (yl >= CUT) & (yl < CUT + LY)
    atoms = LX * LY * DEPTH
    i_col = lax.broadcasted_iota(jnp.int32, (atoms, LANES), 0).astype(F32)
    l_col = lax.broadcasted_iota(jnp.int32, (atoms, LANES), 1).astype(F32)
    rest = i_col - (LY * DEPTH) * jnp.floor((i_col + 0.5) * (1.0 / (LY * DEPTH)))
    y_col = jnp.floor((rest + 0.5) * (1.0 / DEPTH))
    z_col = rest - DEPTH * y_col
    place = jnp.where(l_col == WY * z_col + y_col + HOME, 1.0, 0.0)
    i_row = lax.broadcasted_iota(jnp.int32, (8, atoms), 1).astype(F32)
    x_row = lax.broadcasted_iota(jnp.int32, (8, atoms), 0).astype(F32)
    pick = jnp.floor((i_row + 0.5) * (1.0 / (LY * DEPTH))) == x_row
    for c in loads:
        c.wait()
    raw = [pos_ref[c, 0, 0] for c in range(3)] + [dir_ref[c, 0, 0] for c in range(3)]
    raw += [pol_ref[0, 0], grp_ref[0, 0].astype(F32)]
    stack = jnp.concatenate([jnp.where(pick, jnp.broadcast_to(r, (8, atoms)), 0.0) for r in raw], axis=0)
    spread = jnp.dot(stack, place, precision=lax.Precision.HIGHEST, preferred_element_type=F32)
    field = [spread[8 * k:8 * k + 8] for k in range(8)]
    site = (row.astype(F32), yl - CUT, zl - CUT)
    u = [jnp.where(home, field[c] - site[c], 0.0) for c in range(3)]
    direct = field[3:6]
    pol, group = field[6], field[7]
    d0 = [pol * f for f in direct]

    def pack(parts):
        out = None
        for c, p in enumerate(parts):
            r = lane_roll(p, SPAN * c - HOME)
            out = r if out is None else out + r
        return out

    sbf[0] = pack(u)
    sbf[1] = pack(d0)
    sbf[2] = pack([pol])
    pl.semaphore_wait(barrier, len(partners))

    def halo_copies(k):
        for j, o in enumerate(halo):
            back = at(tuple(-v for v in o))
            if k == 0:
                yield pltpu.make_async_remote_copy(sbf, rbf.at[j], sf_send.at[j], sf_recv.at[j],
                                                   device_id=back, device_id_type=MESH)
            else:
                yield pltpu.make_async_remote_copy(sbv.at[k - 1], rbv.at[k - 1, j], sv_send.at[k - 1, j],
                                                   sv_recv.at[k - 1, j], device_id=back, device_id_type=MESH)

    def start(copies):
        copies = list(copies)
        for c in copies:
            c.start()
        return copies

    def block(k, tile, o):
        c = tuple(canon(v, n) for v, n in zip(o, dims))
        if c == (0, 0, 0):
            return sbf[tile] if k == 0 else sbv[k - 1]
        j = halo.index(c)
        return rbf[j, tile] if k == 0 else rbv[k - 1, j]

    low = row < CUT

    def assemble(k, tile, count, fill=0.0):
        out = [[jnp.full((8, LANES), fill, F32)] * 2 for _ in range(count)]
        done = {}
        for oy in (-1, 0, 1):
            y0, y1 = (0, CUT) if oy < 0 else (CUT, CUT + LY) if oy == 0 else (CUT + LY, WY)
            for oz in (-1, 0, 1):
                key = (oy if ny > 2 else oy % ny, oz if nz > 2 else oz % nz)
                if key not in done:
                    left, mid, right = (pltpu.roll(block(k, tile, (ox, oy, oz)), CUT, axis=0) for ox in (-1, 0, 1))
                    done[key] = (jnp.where(low, left, mid), jnp.where(low, mid, right))
                mask = (zl >= DEPTH * (oz + 1)) & (zl < DEPTH * (oz + 2)) & (yl >= y0) & (yl < y1)
                for c in range(count):
                    shift = SPAN * (oz + 1 - c) + LY * oy + CUT
                    for t in range(2):
                        out[c][t] = jnp.where(mask, lane_roll(done[key][t], shift), out[c][t])
        return out

    def spread_dy(ref, slot, tiles, add_dy=False):
        for dy in range(-CUT, CUT + 1):
            for t in range(2):
                v = lane_roll(tiles[t], -dy)
                ref[dy + CUT, slot, 8 * t:8 * t + 8, :] = v + float(dy) if add_dy else v

    def replicate(v):
        v = jnp.where(home, v, 0.0)
        base = v + lane_roll(v, SPAN) + lane_roll(v, -SPAN)
        return base, lane_roll(base, -WY), lane_roll(base, WY)

    def fold(acc):
        out = None
        for dz in range(-CUT, CUT + 1):
            r = lane_roll(acc[-dz % 3], -WY * dz)
            out = r if out is None else out + r
        return jnp.where(home, out, 0.0)

    def pair_loops(body):
        carry = tuple(jnp.zeros((8, LANES), F32) for _ in range(9))
        base = 0
        for first, step, n, w in LOOPS:
            width = (2 * w + 1) * 3

            def turn(it, carry, first=first, step=step, w=w, width=width, base=base):
                dyi = first + CUT + step * it
                carry = list(carry)
                for j, dx in enumerate(range(-w, w + 1)):
                    for q, add in enumerate(body(dx, dyi, base + it * width + 3 * j)):
                        for c in range(3):
                            carry[3 * q + c] = carry[3 * q + c] + add[c]
                return tuple(carry)

            carry = lax.fori_loop(0, n, turn, carry)
            base += n * width
        return [fold([carry[3 * q + c] for q in range(3)]) for c in range(3)]

    later = []
    copies = start(halo_copies(0))
    dzq = (jnp.where(lane < SPAN, -3.0, jnp.where(lane < 2 * SPAN, 0.0, 3.0)),
           jnp.where(lane < 5 * WY, -1.0, 2.0), jnp.where(lane < 4 * WY, -2.0, 1.0))
    rp = lax.rsqrt(jnp.where(home, pol, 1.0))
    for c, v in enumerate(u + [rp, group]):
        for q, r in enumerate(replicate(v)):
            own[q, c] = r - dzq[q] if c == 2 else r
    far_group = [pltpu.roll(jnp.where(home, group, -1.0), CUT, axis=0)] * 2
    spread_dy(pd, 4, [jnp.where(low, -1.0, far_group[0]), jnp.where(low, far_group[1], -1.0)])
    for c in copies:
        c.wait_recv()
    later.extend(copies)
    for c, tiles in enumerate(assemble(0, 0, 3)):
        spread_dy(pd, c, tiles, add_dy=c == 1)
    far_pol = assemble(0, 2, 1, 1.0)[0]
    spread_dy(pd, 3, [lax.rsqrt(jnp.where(t > 0.0, t, 1.0)) for t in far_pol])

    def keep(k, parts):
        for c, tiles in enumerate(parts):
            for t in range(2):
                vpad[k, c, t] = tiles[t]

    def ghosts(k):
        parts = assemble(k, 1 if k == 0 else 0, 3)
        keep(k, parts)
        for c in range(3):
            spread_dy(vd, c, parts[c])

    def rows(ref, dyi, slot, dx):
        return ref[dyi, slot, CUT + dx:CUT + dx + 8, :]

    def mul(t, v):
        xx, xy, xz, yy, yz, zz = t
        return (xx * v[0] + xy * v[1] + xz * v[2], xy * v[0] + yy * v[1] + yz * v[2],
                xz * v[0] + yz * v[1] + zz * v[2])

    def build(dx, dyi, index):
        far = [rows(pd, dyi, c, dx) for c in range(5)]
        v = [rows(vd, dyi, c, dx) for c in range(3)]
        out = []
        for q in range(3):
            ex = far[0] - own[q, 0] + float(dx)
            ey = far[1] - own[q, 1]
            ez = far[2] - own[q, 2]
            s = ex * ex + ey * ey + ez * ez
            same = s < 0.01
            maybe_self = dx == 0 and q == 0
            if maybe_self:
                s = jnp.where(same, 1.0, s)
            inv = lax.rsqrt(s)
            tap = jnp.maximum(1.0 - s * (1.0 / (CUT * CUT)), 0.0)
            x = (0.39 * s) * (s * inv) * (far[3] * own[q, 3])
            e = jnp.exp(-x)
            xe = x * e
            l3 = 1.0 - e
            l5 = l3 - xe
            inv2 = inv * inv
            g = jnp.where(far[4] == own[q, 4], 0.5, 1.0) * (inv2 * inv)
            if maybe_self:
                g = jnp.where(same, 0.0, g)
            gt = g * tap
            gi = 3.0 * gt * inv2
            gl = gt * l3
            c3 = gl * tap
            c5 = gi * tap * l5
            h3 = (-4.0 / (CUT * CUT)) * gl - c5
            h5 = gi * ((-4.0 / (CUT * CUT)) * l5 + tap * inv2 * (3.0 * x * xe - 5.0 * l5))
            fx, fy, fz = c5 * ex, c5 * ey, c5 * ez
            t = (fx * ex - c3, fx * ey, fx * ez, fy * ey - c3, fy * ez, fz * ez - c3)
            for k, value in enumerate(t + (ex, ey, ez, c5, h3, h5)):
                tab[k, index + q] = value
            out.append(mul(t, v))
        return out

    def apply(dx, dyi, index):
        v = [rows(vd, dyi, c, dx) for c in range(3)]
        return [mul([tab[k, index + q] for k in range(6)], v) for q in range(3)]

    def place_in(o, axes):
        p, out = at(o), 0
        for a in axes:
            out = out * dims[a] + p[a]
        return out

    def send_sum(r, axes, offsets, src, dst, send, recv):
        mine = place_in((0, 0, 0), axes)
        copies = start(
            pltpu.make_async_remote_copy(src.at[r], dst.at[r, mine], send.at[r, j], recv.at[r, mine],
                                         device_id=at(o), device_id_type=MESH)
            for j, o in enumerate(offsets))
        dst[r, mine] = src[r]
        return copies

    def take_sum(r, axes, offsets, src, dst, send, recv):
        for j, o in enumerate(offsets):
            place = place_in(o, axes)
            pltpu.make_async_remote_copy(src.at[r], dst.at[r, place], send.at[r, j], recv.at[r, place],
                                         device_id=at(o), device_id_type=MESH).wait_recv()
        terms = [dst[r, k] for k in range(len(offsets) + 1)]
        while len(terms) > 1:
            terms = [sum(terms[k:k + 2][1:], terms[k]) for k in range(0, len(terms), 2)]
        return terms[0]

    one = (first, plane, rsb, red, r_send, r_recv)
    two = (second, column, rsb2, red2, q_send, q_recv)
    lane1 = lax.broadcasted_iota(jnp.int32, (1, LANES), 1)

    def begin_sum(r, values):
        tile = jnp.zeros((1, LANES), F32)
        for k, v in enumerate(values):
            total = jnp.sum(jnp.sum(v, axis=0, keepdims=True), axis=1, keepdims=True)
            tile = jnp.where(lane1 == k, total, tile)
        rsb[r] = tile
        later.extend(send_sum(r, *one))

    def middle_sum(r):
        if column:
            rsb2[r] = take_sum(r, *one)
            later.extend(send_sum(r, *two))

    def end_sum(r, count):
        total = take_sum(r, *(two if column else one))
        return [jnp.sum(jnp.where(lane1 == k, total, 0.0), axis=1, keepdims=True) for k in range(count)]

    def inner(a, b):
        return a[0] * b[0] + a[1] * b[1] + a[2] * b[2]

    ghosts(0)
    r0 = pair_loops(build)
    z0 = [pol * v for v in r0]
    sbv[0] = pack(z0)
    copies = start(halo_copies(1))
    for c in copies:
        c.wait_recv()
    later.extend(copies)
    ghosts(1)
    t1 = pair_loops(apply)
    z2 = [pol * v for v in t1]
    sbv[1] = pack(z2)
    copies = start(halo_copies(2))
    image0 = [a - b for a, b in zip(r0, t1)]
    begin_sum(0, [inner(r0, z0), inner(z0, image0), inner(d0, direct), inner(z0, direct)])
    middle_sum(0)
    for c in copies:
        c.wait_recv()
    later.extend(copies)
    ghosts(2)
    t2 = pair_loops(apply)
    sbv[2] = pack([pol * v for v in t2])
    copies = start(halo_copies(3))
    norm0, curve0, e_d0, e_z0 = end_sum(0, 4)
    gamma0 = norm0 / curve0
    r1 = [a - gamma0 * b for a, b in zip(r0, image0)]
    z1 = [pol * v for v in r1]
    tz1 = [a - gamma0 * (a - b) for a, b in zip(t1, t2)]
    az1 = [a - b for a, b in zip(r1, tz1)]
    begin_sum(1, [inner(r1, z1), inner(z1, az1), inner(z1, image0), inner(z1, direct)])
    middle_sum(1)
    for c in copies:
        c.wait_recv()
    later.extend(copies)
    keep(3, assemble(3, 0, 3))
    norm1, az11, az01, e_z1 = end_sum(1, 4)
    beta = norm1 / norm0
    curve1 = az11 + 2.0 * beta * az01 + beta * beta * curve0
    gamma1 = norm1 / curve1
    energy = -(e_d0 + gamma0 * e_z0 + gamma1 * (e_z1 + beta * e_z0)) * (1.0 / (2.0 * atoms * devices))
    en_ref[...] = energy
    stores = [pltpu.make_async_copy(en_ref, en_hbm, io_sem.at[4])]

    own_p, own_a = [], []
    dip = []
    for c in range(3):
        dip.append(d0[c] + gamma0 * z0[c] + gamma1 * (z1[c] + beta * z0[c]))
        tiles_p, tiles_a = [], []
        for t in range(2):
            g0, g1, g2, g3 = (vpad[k, c, t] for k in range(4))
            f1 = g1 - gamma0 * (g1 - g2)
            f2 = g2 - gamma0 * (g2 - g3)
            tiles_p.append(g0 + gamma0 * g1 + gamma1 * (f1 + beta * g1))
            tiles_a.append(g0 + g1 + gamma0 * g2 + gamma1 * (f2 + beta * g2))
        spread_dy(vd, c, tiles_p)
        spread_dy(vd, 3 + c, tiles_a)
        for q, r in enumerate(replicate(dip[c])):
            own[q, 5 + c] = r
        for q, r in enumerate(replicate(vd[CUT, 3 + c, CUT:CUT + 8, :])):
            own[q, 8 + c] = r

    def slope(dx, dyi, index):
        fp = [rows(vd, dyi, c, dx) for c in range(3)]
        fa = [rows(vd, dyi, 3 + c, dx) for c in range(3)]
        out = []
        for q in range(3):
            op = [own[q, 5 + c] for c in range(3)]
            oa = [own[q, 8 + c] for c in range(3)]
            d = [tab[DX + c, index + q] for c in range(3)]
            opd, oad, fpd, fad = inner(op, d), inner(oa, d), inner(fp, d), inner(fa, d)
            cross = inner(op, fa) + inner(oa, fp)
            radial = tab[H5, index + q] * (opd * fad + oad * fpd) - tab[H3, index + q] * cross
            c5 = tab[C5, index + q]
            out.append(tuple(
                d[c] * radial + c5 * (op[c] * fad + fa[c] * opd + oa[c] * fpd + fp[c] * oad) for c in range(3)))
        return out

    def put(parts, ref):
        result = lax.dot_general(jnp.concatenate(parts, axis=0), place, (((1,), (1,)), ((), ())),
                                 precision=lax.Precision.HIGHEST, preferred_element_type=F32)
        for c in range(3):
            ref[c, 0, 0] = jnp.sum(jnp.where(pick, result[8 * c:8 * c + 8], 0.0), axis=0, keepdims=True)

    put(dip, dip_ref)
    stores.append(pltpu.make_async_copy(dip_ref, dip_hbm, io_sem.at[5]))
    for c in stores:
        c.start()
    grad = [-0.5 * v for v in pair_loops(slope)]
    put(grad, grad_ref)
    stores.append(pltpu.make_async_copy(grad_ref, grad_hbm, io_sem.at[6]))
    stores[-1].start()
    for c in later:
        c.wait_send()
    for c in stores:
        c.wait()


def solution(mesh):
    dims = tuple(mesh.shape[a] for a in ("gx", "gy", "gz"))
    devices = dims[0] * dims[1] * dims[2]

    def on_device(positions, polarizability, direct_field, groups):
        h = len(halo_offsets(dims))
        plane, column = (group_size(dims, axes) for axes in sum_groups(dims))
        dma = pltpu.SemaphoreType.DMA
        hbm = pl.BlockSpec(memory_space=pl.ANY)
        both, energy = pl.pallas_call(
            functools.partial(kernel, dims, devices),
            out_shape=(jax.ShapeDtypeStruct((6,) + positions.shape[1:], F32),
                       jax.ShapeDtypeStruct((1, 1), F32)),
            in_specs=[hbm] * 4,
            out_specs=(hbm, hbm),
            scratch_shapes=[
                *(pltpu.VMEM(v.shape, v.dtype) for v in (positions, polarizability, direct_field, groups)),
                pltpu.VMEM(positions.shape, F32), pltpu.VMEM(positions.shape, F32), pltpu.VMEM((1, 1), F32),
                dma((7,)),
                pltpu.VMEM((3, 8, LANES), F32),
                pltpu.VMEM((EXCH - 1, 8, LANES), F32),
                pltpu.VMEM((h, 3, 8, LANES), F32),
                pltpu.VMEM((EXCH - 1, h, 8, LANES), F32),
                pltpu.VMEM((2, plane, 1, LANES), F32),
                pltpu.VMEM((EXCH, 3, 2, 8, LANES), F32),
                pltpu.VMEM((7, 6, 16, LANES), F32),
                pltpu.VMEM((7, 5, 16, LANES), F32),
                pltpu.VMEM((3, 11, 8, LANES), F32),
                pltpu.VMEM((12, PAIRS, 8, LANES), F32),
                dma((h,)), dma((h,)), dma((EXCH - 1, h)), dma((EXCH - 1, h)),
                dma((2, plane)), dma((2, plane)), dma((2, column)), dma((2, column)),
                pltpu.VMEM((2, column, 1, LANES), F32),
                pltpu.VMEM((2, 1, LANES), F32), pltpu.VMEM((2, 1, LANES), F32),
            ],
            compiler_params=pltpu.CompilerParams(collective_id=0, has_side_effects=True),
        )(positions, polarizability, direct_field, groups)
        return both[:3], both[3:], energy.reshape(())

    vec, one = P(None, "gx", "gy", "gz", None), P("gx", "gy", "gz", None)
    return jax.shard_map(on_device, mesh=mesh, in_specs=(vec, one, vec, one), out_specs=(vec, vec, P()),
                         check_vma=False)
```
